32 devices in a mesh: row: 4 (over y, x), col: 8 (over z, core).
Axes of the slice: x: 2, y: 2, z: 4, core: 2. Of those that a mesh axis runs over, the one named last changes fastest.
Arguments:
- vectors: float32 [32, 32768], P(None, ('row', 'col'))
- tiles: float32 [4096, 128, 128], P(('row', 'col'))
- tile_row: int32 [32, 128], P(('row', 'col')), may hold values from 0 to 63, never falling along the last dimension, each value on 1 to 6 neighbouring positions
- tile_col: int32 [32, 128], P(('row', 'col')), may hold values from 0 to 31
Outputs:
- filtered: float32 [32, 32768], P(None, ('row', 'col'))
- gram: float32 [32, 32], replicated
The draws below stay inside these ranges and needn't reach their ends.
Inputs may be any that keep to these rules, and one draw needn't show every extreme that they name: `tile_row`: on each device the entries never fall along the last dimension, and each of the 64 values is taken by 1 to 6 slots.
All inputs are finite; a program needn't handle non-finite values.
Results may differ from the reference program's by a relative error of at most 0.00015.
Values sent between devices are 32-bit elements; how exact they have to be, the bound alone decides.
No kernel may reach another device: no remote copies, remote signals or barrier semaphores. Data moves between devices by JAX's collectives and lax.ppermute only.
A program may use at most 64 MiB of HBM per device.

```python
import math
import jax
import jax.numpy as jnp
import numpy as np
from jax import lax

TB = 128
K = 32
STEPS = 3
TILE_RATE = 2
BLK_DEV = 8
LOCAL_ROWS = 64
LOCAL_COLS = 32
TILES_DEV = 128
SLOTS = 4096
ROWS = 32768
N_ROW = 4
N_COL = 8


def draw_tiles(key, part):
    first, second, third = jax.random.split(key, 3)
    base = jax.random.normal(first, (SLOTS, TB, TB), jnp.float32) + 1.0
    row_scale = jnp.exp(jax.random.uniform(second, (SLOTS, TB, 1), jnp.float32, 0.0, math.log(10.0)))
    col_scale = jnp.exp(jax.random.uniform(third, (SLOTS, 1, TB), jnp.float32, 0.0, math.log(3.0)))
    return base * row_scale * col_scale


def draw_vectors(key, part):
    first, second, third = jax.random.split(key, 3)
    noise = jax.random.normal(first, (K, ROWS), jnp.float32)
    amplitude = 0.4 * jax.random.normal(second, (K, 1), jnp.float32)
    profile = jnp.exp(jax.random.uniform(third, (1, ROWS), jnp.float32, 0.0, math.log(4.0)))
    return noise + amplitude * profile


def set_ends(result, own_key, low, top_value):
    longest = result.shape.index(max(result.shape))
    spots = []
    for shift in (0, 1):
        where = [jax.random.randint(jax.random.fold_in(own_key, axis), (), 0, length) for axis, length in enumerate(result.shape)]
        where[longest] = (where[longest] + shift) % result.shape[longest]
        spots.append(tuple(where))
    return result.at[spots[0]].set(low).at[spots[1]].set(top_value)


def split_up(count, total, most, slope):
    loads = [(1 << 20) // math.isqrt(rank ** slope) + 1 for rank in range(2, count + 1)]
    spare, given = total - most - (count - 1), [1] * (count - 1)
    while spare > 0:
        candidates = [i for i in range(count - 1) if given[i] < most]
        mass, remaining = sum([loads[i] for i in candidates]), spare
        for i in candidates:
            extra = min(most - given[i], max(1, remaining * loads[i] // mass), spare)
            given[i] = given[i] + extra
            spare = spare - extra
    return np.array([most] + given)


def uneven(rng, number_of, total, limit, skew):
    if number_of == 2:
        one = jax.random.randint(rng, (), max(1, total - limit), min(limit, total - 1) + 1)
        return jnp.stack([one, total - one])
    sizes = jnp.asarray(split_up(number_of, total, limit, skew), jnp.int32)
    twos = (number_of - 1) // 2
    donor, sink = sizes[1:1 + 2 * twos:2], sizes[2:2 + 2 * twos:2]
    slack = jnp.minimum(donor - 1, limit - sink)
    passed = jax.random.randint(jax.random.fold_in(rng, 1), (twos,), 0, 1 << 20) % (slack + 1)
    sizes = sizes.at[1:1 + 2 * twos:2].set(donor - passed).at[2:2 + 2 * twos:2].set(sink + passed)
    return sizes[jax.random.permutation(jax.random.fold_in(rng, 2), number_of)]


def setup_inputs(seed: int = 0) -> dict:
    splits = jax.random.split(jax.random.key(seed), 5)
    vectors = draw_vectors(jax.random.fold_in(splits[4], 71), 0)
    tiles = draw_tiles(jax.random.fold_in(splits[4], 71), 0)
    tile_row = jax.vmap(lambda own: jnp.searchsorted(jnp.cumsum(uneven(own, LOCAL_ROWS, TILES_DEV, 3 * TILE_RATE, 2)), jnp.arange(TILES_DEV), side="right"))(jax.random.split(splits[2], (N_ROW * N_COL))).reshape((N_ROW * N_COL, TILES_DEV)).astype(jnp.int32)
    tile_col = set_ends(jax.random.randint(splits[3], (N_ROW * N_COL, TILES_DEV), 0, LOCAL_COLS), jax.random.fold_in(splits[3], 1), 0, LOCAL_COLS - 1).astype(jnp.int32)
    return dict(vectors=vectors, tiles=tiles, tile_row=tile_row, tile_col=tile_col)


def reference(vectors, tiles, tile_row, tile_col):
    devices = jnp.arange(N_ROW * N_COL, dtype=jnp.int32)[:, None]
    row_index = devices // N_COL
    col_index = devices % N_COL
    global_row = (row_index * LOCAL_ROWS + tile_row).reshape(-1).astype(jnp.int32)
    global_col = ((tile_col // BLK_DEV * N_COL + col_index) * BLK_DEV + tile_col % BLK_DEV).reshape(-1).astype(jnp.int32)
    blocks = N_ROW * N_COL * BLK_DEV
    magnitude = lax.optimization_barrier(jnp.sum(jnp.abs(tiles), axis=2))
    degree = 1.0 + jax.ops.segment_sum(magnitude, global_row, num_segments=blocks).reshape(-1)
    scale = 1.0 / jnp.sqrt(degree)

    def operate(current):
        scaled = (current * scale[None, :]).reshape(K, blocks, TB)
        picked = jnp.take(scaled, global_col, axis=1)
        product = jnp.einsum('tij,ktj->tki', tiles, picked, precision=lax.Precision.HIGHEST)
        summed = jax.ops.segment_sum(product, global_row, num_segments=blocks)
        return jnp.transpose(summed, (1, 0, 2)).reshape(K, blocks * TB) * scale[None, :]
    previous = vectors
    current = operate(vectors)
    for step in range(STEPS - 1):
        following = 2.0 * operate(current) - previous
        previous = current
        current = following
    gram = jnp.dot(current, current.T, precision=lax.Precision.HIGHEST) / ROWS
    return (current, gram)
```

```python
import functools

import jax
import jax.numpy as jnp
from jax import lax
from jax.experimental import pallas as pl
from jax.experimental.pallas import tpu as pltpu
from jax.sharding import PartitionSpec as P

TB = 128
STEPS = 3
GROUP = 16


def split_kernel(rows, tiles_ref, pair_ref, terms_ref, carry):
    step = pl.program_id(0)
    group = tiles_ref.shape[0]
    ones = jnp.ones((16, 2 * TB), jnp.bfloat16)

    @pl.when(step == 0)
    def _():
        carry[...] = jnp.zeros_like(carry)

    total = carry[...]
    for t in range(group):
        index = step * group + t
        row = rows[index]
        same = jnp.logical_and(index > 0, row == rows[jnp.maximum(index - 1, 0)])
        tile = tiles_ref[t]
        high = tile.astype(jnp.bfloat16)
        low = (tile - high.astype(jnp.float32)).astype(jnp.bfloat16)
        pair_ref[t, :, 0:TB] = high
        pair_ref[t, :, TB : 2 * TB] = low
        size = jnp.abs(tile)
        size_high = size.astype(jnp.bfloat16)
        size_low = (size - size_high.astype(jnp.float32)).astype(jnp.bfloat16)
        sums = lax.dot_general(
            ones,
            jnp.concatenate([size_high, size_low], axis=1),
            (((1,), (1,)), ((), ())),
            preferred_element_type=jnp.float32,
        )
        total = sums[0:8] + jnp.where(same, total, 0.0)
        terms_ref[pl.ds(row, 1), :] = total[0:1]
    carry[...] = total


def split_tiles(tiles, rows, local_rows):
    count = tiles.shape[0]
    return pl.pallas_call(
        split_kernel,
        out_shape=(
            jax.ShapeDtypeStruct((count, TB, 2 * TB), jnp.bfloat16),
            jax.ShapeDtypeStruct((local_rows, TB), jnp.float32),
        ),
        grid_spec=pltpu.PrefetchScalarGridSpec(
            num_scalar_prefetch=1,
            grid=(count // GROUP,),
            in_specs=[pl.BlockSpec((GROUP, TB, TB), lambda i, rows: (i, 0, 0))],
            out_specs=[
                pl.BlockSpec((GROUP, TB, 2 * TB), lambda i, rows: (i, 0, 0)),
                pl.BlockSpec((local_rows, TB), lambda i, rows: (0, 0)),
            ],
            scratch_shapes=[pltpu.VMEM((8, TB), jnp.float32)],
        ),
        compiler_params=pltpu.CompilerParams(vmem_limit_bytes=24 << 20),
        cost_estimate=pl.CostEstimate(
            flops=count * TB * TB * 64, bytes_accessed=count * TB * TB * 8, transcendentals=0
        ),
        name="split_tiles",
    )(rows, tiles)


def product_kernel(n_row, n_col, owned, rows, cols, place, *refs):
    sources = refs[:n_row]
    terms_ref, pair_ref, keep_ref, give_ref, scale_ref, operand, sums, carry = refs[n_row:]
    step = pl.program_id(0)
    group = pair_ref.shape[0]
    k = sources[0].shape[0]
    a, b = place[0], place[1]

    @pl.when(step == 0)
    def _():
        carry[...] = jnp.zeros_like(carry)
        for s in range(n_row):
            degree = 1.0 + jnp.sum(terms_ref[a ^ s], axis=0)
            scale = 1.0 / jnp.sqrt(degree)
            for o in range(owned):
                at = slice(o * TB, (o + 1) * TB)
                if s == 0:
                    scale_ref[:, at] = scale[o : o + 1]
                value = sources[s][:, at] * scale[o : o + 1]
                high = value.astype(jnp.bfloat16)
                low = (value - high.astype(jnp.float32)).astype(jnp.bfloat16)
                operand[s * owned + o, 0:k, 0:TB] = high
                operand[s * owned + o, 0:k, TB : 2 * TB] = high
                operand[s * owned + o, k : 2 * k, 0:TB] = low
                operand[s * owned + o, k : 2 * k, TB : 2 * TB] = low

    total = carry[...]
    for t in range(group):
        index = step * group + t
        row, col = rows[index], cols[index]
        same = jnp.logical_and(index > 0, row == rows[jnp.maximum(index - 1, 0)])
        where_from = (lax.div(col, owned) ^ a) * owned + lax.rem(col, owned)
        where_to = (lax.div(row, owned) ^ b) * owned + lax.rem(row, owned)
        both = lax.dot_general(
            operand[where_from],
            pair_ref[t],
            (((1,), (1,)), ((), ())),
            preferred_element_type=jnp.float32,
        )
        total = both[0:k] + both[k : 2 * k] + jnp.where(same, total, 0.0)
        sums[where_to] = total
    carry[...] = total

    @pl.when(step == pl.num_programs(0) - 1)
    def _():
        for d in range(n_col):
            out = give_ref if d % 2 else keep_ref
            for o in range(owned):
                out[d // 2, :, o * TB : (o + 1) * TB] = sums[d * owned + o]


def products(sources, terms, pairs, rows, cols, place, n_row, n_col):
    k, width = sources[0].shape
    owned = width // TB
    count = pairs.shape[0]
    half = jax.ShapeDtypeStruct((n_col // 2, k, width), jnp.float32)
    whole = lambda shape: pl.BlockSpec(shape, lambda i, *_: (0,) * len(shape))
    return pl.pallas_call(
        functools.partial(product_kernel, n_row, n_col, owned),
        out_shape=(half, half, jax.ShapeDtypeStruct((1, width), jnp.float32)),
        grid_spec=pltpu.PrefetchScalarGridSpec(
            num_scalar_prefetch=3,
            grid=(count // GROUP,),
            in_specs=[whole((k, width))] * n_row
            + [
                whole(terms.shape),
                pl.BlockSpec((GROUP, TB, 2 * TB), lambda i, *_: (i, 0, 0)),
            ],
            out_specs=[whole(half.shape)] * 2 + [whole((1, width))],
            scratch_shapes=[
                pltpu.VMEM((n_row * owned, 2 * k, 2 * TB), jnp.bfloat16),
                pltpu.VMEM((n_col * owned, k, TB), jnp.float32),
                pltpu.VMEM((k, TB), jnp.float32),
            ],
        ),
        compiler_params=pltpu.CompilerParams(vmem_limit_bytes=32 << 20),
        cost_estimate=pl.CostEstimate(
            flops=count * TB * TB * 2 * k * 4,
            bytes_accessed=count * TB * TB * 4,
            transcendentals=0,
        ),
        name="products",
    )(rows, cols, place, *sources, terms, pairs)


def swap(value, axis, size, by):
    return lax.ppermute(value, axis, [(i, i ^ by) for i in range(size)])


def on_device(vectors, tiles, tile_row, tile_col):
    rows, cols = tile_row[0], tile_col[0]
    n_row = lax.axis_size("row")
    n_col = lax.axis_size("col")
    k, width = vectors.shape
    owned = width // TB
    local_rows = n_col * owned
    a, b = lax.axis_index("row"), lax.axis_index("col")
    place = jnp.stack([a, b]).astype(jnp.int32)

    def spread(value):
        return [value] + [swap(value, "row", n_row, s) for s in range(1, n_row)]

    sources = spread(vectors)
    pairs, terms = split_tiles(tiles, rows, local_rows)
    sent = jnp.broadcast_to(
        terms.reshape(1, n_col, owned, TB), (n_row, n_col, owned, TB)
    ).reshape(n_row * n_col, owned, TB)
    got = lax.all_to_all(sent, ("row", "col"), 0, 0, tiled=True)
    got = got.reshape(n_row, n_col, owned, TB)

    previous, current = None, vectors
    for step in range(STEPS):
        keep, give, scale = products(sources, got, pairs, rows, cols, place, n_row, n_col)
        chip = keep + swap(give, "col", n_col, 1)
        total = chip[0]
        for d in range(1, n_col // 2):
            total = total + swap(chip[d], "col", n_col, 2 * d)
        if step == 0:
            following = total * scale
        else:
            following = 2.0 * (total * scale) - previous
        previous, current = current, following
        if step < STEPS - 1:
            sources = spread(current)

    local_gram = jnp.dot(current, current.T, precision=lax.Precision.HIGHEST)
    devices = n_row * n_col
    grams = lax.all_to_all(
        jnp.broadcast_to(local_gram[None], (devices, k, k)), ("row", "col"), 0, 0, tiled=True
    )
    gram = jnp.sum(grams, axis=0) / (width * devices)
    return (current, gram)


def solution(mesh):
    in_specs = (
        P(None, ("row", "col")),
        P(("row", "col"), None, None),
        P(("row", "col"), None),
        P(("row", "col"), None),
    )
    out_specs = (P(None, ("row", "col")), P())
    return jax.shard_map(
        on_device, mesh=mesh, in_specs=in_specs, out_specs=out_specs, check_vma=False
    )
```

```python
import functools

import jax
import jax.numpy as jnp
from jax import lax
from jax.experimental import pallas as pl
from jax.experimental.pallas import tpu as pltpu
from jax.sharding import PartitionSpec as P

TB = 128
STEPS = 3
GROUP = 16
UNROLL = 32
CHUNKS = 1

SCALARS = pl.BlockSpec(memory_space=pltpu.SMEM)
VECTORS = pl.BlockSpec(memory_space=pltpu.VMEM)


def same_row(rows, index):
    return jnp.logical_and(index > 0, rows[index] == rows[jnp.maximum(index - 1, 0)])


def two_parts(value):
    high = value.astype(jnp.bfloat16)
    return high, (value - high.astype(jnp.float32)).astype(jnp.bfloat16)


def degree_kernel(rows, tiles_hbm, sent_ref, buffer, terms, arrived):
    count = tiles_hbm.shape[0]
    groups = count // GROUP
    ones = jnp.ones((16, 2 * TB), jnp.bfloat16)

    def fetch(group):
        at = pl.ds(group * GROUP, GROUP)
        return pltpu.make_async_copy(tiles_hbm.at[at], buffer.at[at], arrived.at[group])

    for group in range(groups):
        fetch(group).start()

    def body(group, total):
        fetch(group).wait()
        for t in range(GROUP):
            index = group * GROUP + t
            sums = lax.dot_general(
                ones,
                jnp.concatenate(two_parts(jnp.abs(buffer[index])), axis=1),
                (((1,), (1,)), ((), ())),
                preferred_element_type=jnp.float32,
            )
            total = sums[0:8] + jnp.where(same_row(rows, index), total, 0.0)
            terms[pl.ds(rows[index], 1), :] = total[0:1]
        return total

    lax.fori_loop(0, groups, body, jnp.zeros((8, TB), jnp.float32))
    n_row, n_col, owned, _ = sent_ref.shape
    for s in range(n_row):
        for d in range(n_col):
            sent_ref[s, d] = terms[d * owned : (d + 1) * owned]


def degree_terms(tiles, rows, n_row, n_col, owned):
    count = tiles.shape[0]
    return pl.pallas_call(
        degree_kernel,
        out_shape=jax.ShapeDtypeStruct((n_row, n_col, owned, TB), jnp.float32),
        in_specs=[SCALARS, pl.BlockSpec(memory_space=pltpu.HBM)],
        out_specs=VECTORS,
        scratch_shapes=[
            pltpu.VMEM(tiles.shape, jnp.float32),
            pltpu.VMEM((n_col * owned, TB), jnp.float32),
            pltpu.SemaphoreType.DMA((count // GROUP,)),
        ],
        compiler_params=pltpu.CompilerParams(vmem_limit_bytes=24 << 20),
        cost_estimate=pl.CostEstimate(
            flops=count * TB * TB * 64, bytes_accessed=count * TB * TB * 4, transcendentals=0
        ),
        name="degree_terms",
    )(rows, pltpu.with_memory_space_constraint(tiles, pltpu.HBM))


def product_kernel(n_row, n_col, owned, load, rows, cols, place, *refs):
    refs = list(refs)
    take = lambda n: [refs.pop(0) for _ in range(n)]
    sources = [take(CHUNKS) for _ in range(n_row)]
    terms_ref, tiles_from = take(2)
    keeps, gives = take(CHUNKS), take(CHUNKS)
    (scale_ref,) = take(1)
    tiles_ref = refs.pop(0) if load else tiles_from
    operand, sums = take(2)
    count = tiles_ref.shape[0]
    part = keeps[0].shape[1]
    k = part * CHUNKS
    a, b = place[0], place[1]

    def fetch(group):
        at = pl.ds(group * UNROLL, UNROLL)
        return pltpu.make_async_copy(tiles_from.at[at], tiles_ref.at[at], refs[0].at[group])

    if load:
        for group in range(count // UNROLL):
            fetch(group).start()
    for s in range(n_row):
        degree = 1.0 + jnp.sum(terms_ref[a ^ s], axis=0)
        scale = 1.0 / jnp.sqrt(degree)
        for o in range(owned):
            at = slice(o * TB, (o + 1) * TB)
            if s == 0:
                scale_ref[:, at] = scale[o : o + 1]
            for c in range(CHUNKS):
                high, low = two_parts(sources[s][c][:, at] * scale[o : o + 1])
                for first, value in ((c * part, high), (k + c * part, low)):
                    operand[s * owned + o, first : first + part, 0:TB] = value
                    operand[s * owned + o, first : first + part, TB : 2 * TB] = value

    def body(group, total):
        if load:
            fetch(group).wait()
        for t in range(UNROLL):
            index = group * UNROLL + t
            row, col = rows[index], cols[index]
            where_from = (lax.div(col, owned) ^ a) * owned + lax.rem(col, owned)
            where_to = (lax.div(row, owned) ^ b) * owned + lax.rem(row, owned)
            both = lax.dot_general(
                operand[where_from],
                jnp.concatenate(two_parts(tiles_ref[index]), axis=1),
                (((1,), (1,)), ((), ())),
                preferred_element_type=jnp.float32,
            )
            total = both[0:k] + both[k : 2 * k] + jnp.where(same_row(rows, index), total, 0.0)
            sums[where_to] = total
        return total

    lax.fori_loop(0, count // UNROLL, body, jnp.zeros((k, TB), jnp.float32))
    half = n_col // 2
    for d in range(n_col):
        at = d % 2 * half + d // 2
        outs = keeps if at < half else gives
        for o in range(owned):
            for c in range(CHUNKS):
                outs[c][at % half, :, o * TB : (o + 1) * TB] = sums[
                    d * owned + o, c * part : (c + 1) * part
                ]


def products(sources, terms, tiles, rows, cols, place, n_row, n_col, load):
    part, width = sources[0].shape
    k = part * CHUNKS
    owned = width // TB
    count = tiles.shape[0]
    half = jax.ShapeDtypeStruct((n_col // 2, part, width), jnp.float32)
    loaded = [jax.ShapeDtypeStruct(tiles.shape, tiles.dtype)] * load
    if load:
        tiles = pltpu.with_memory_space_constraint(tiles, pltpu.HBM)
    outs = pl.pallas_call(
        functools.partial(product_kernel, n_row, n_col, owned, load),
        out_shape=[half] * (2 * CHUNKS)
        + [jax.ShapeDtypeStruct((1, width), jnp.float32)]
        + loaded,
        in_specs=[SCALARS] * 3
        + [VECTORS] * (n_row * CHUNKS + 1)
        + [pl.BlockSpec(memory_space=pltpu.HBM) if load else VECTORS],
        out_specs=[VECTORS] * (2 * CHUNKS + 1 + load),
        scratch_shapes=[
            pltpu.VMEM((n_row * owned, 2 * k, 2 * TB), jnp.bfloat16),
            pltpu.VMEM((n_col * owned, k, TB), jnp.float32),
        ]
        + [pltpu.SemaphoreType.DMA((count // UNROLL,))] * load,
        compiler_params=pltpu.CompilerParams(vmem_limit_bytes=24 << 20),
        cost_estimate=pl.CostEstimate(
            flops=count * TB * TB * 2 * k * 4,
            bytes_accessed=count * TB * TB * 4,
            transcendentals=0,
        ),
        name="products",
    )(rows, cols, place, *sources, terms, tiles)
    return outs[:CHUNKS], outs[CHUNKS : 2 * CHUNKS], *outs[2 * CHUNKS :]


def gram_kernel(mean, *refs):
    *values, out_ref = refs
    value = jnp.concatenate([ref[...] for ref in values], axis=0)
    parts = jnp.concatenate(two_parts(value), axis=0)
    gram = lax.dot_general(
        parts, parts, (((1,), (1,)), ((), ())), preferred_element_type=jnp.float32
    )
    k = value.shape[0]
    gram = mean * (gram[:k, :k] + (gram[:k, k:] + gram[k:, :k]) + gram[k:, k:])
    rows = out_ref.shape[1]
    packed = jnp.concatenate(
        [gram[q * rows : (q + 1) * rows] for q in range(gram.shape[0] // rows)], axis=1
    )
    for d in range(out_ref.shape[0]):
        out_ref[d] = packed


def gram_sum_kernel(parts_ref, out_ref):
    total = jnp.sum(parts_ref[...], axis=0)
    k = out_ref.shape[0]
    rows = total.shape[0]
    for q in range(k // rows):
        out_ref[q * rows : (q + 1) * rows, :] = total[:, q * k : (q + 1) * k]


def swap(value, axis, size, by):
    return lax.ppermute(value, axis, [(i, i ^ by) for i in range(size)])


def on_device(vectors, tiles, tile_row, tile_col):
    rows, cols = tile_row[0], tile_col[0]
    n_row = lax.axis_size("row")
    n_col = lax.axis_size("col")
    devices = n_row * n_col
    k, width = vectors.shape
    owned = width // TB
    part = k // CHUNKS
    chunks = range(CHUNKS)
    place = jnp.stack([lax.axis_index("row"), lax.axis_index("col")]).astype(jnp.int32)

    def spread(value):
        return [value] + [swap(value, "row", n_row, s) for s in reversed(range(1, n_row))][::-1]

    gathered = spread(vectors)
    sent = degree_terms(tiles, rows, n_row, n_col, owned)
    sent, gathered = lax.optimization_barrier((sent, gathered))
    terms = lax.all_to_all(
        sent.reshape(devices, owned, TB), ("row", "col"), 0, 0, tiled=True
    ).reshape(n_row, n_col, owned, TB)

    cut = lambda value: [value[c * part : (c + 1) * part] for c in chunks]
    sources = sum([cut(value) for value in gathered], [])
    current, previous = cut(vectors), None
    for step in range(STEPS):
        keeps, gives, scale, *loaded = products(
            sources, terms, tiles, rows, cols, place, n_row, n_col, step == 0
        )
        if loaded:
            tiles = loaded[0]
        chips = [keeps[c] + swap(gives[c], "col", n_col, 1) for c in chunks]
        taken = [
            [chips[c][0]]
            + [swap(chips[c][j], "col", n_col, 2 * j) for j in reversed(range(1, n_col // 2))]
            for c in chunks
        ]
        following, spreads = [], []
        for c in chunks:
            terms_here = taken[c]
            if spreads:
                terms_here, spreads[-1] = lax.optimization_barrier((terms_here, spreads[-1]))
            value = sum(terms_here[1:], terms_here[0]) * scale
            if step > 0:
                value = 2.0 * value - previous[c]
            following.append(value)
            if step < STEPS - 1:
                spreads.append(spread(value))
        previous, current = current, following
        if step < STEPS - 1:
            sources = [spreads[c][s] for s in range(n_row) for c in chunks]

    packed = jax.ShapeDtypeStruct((devices, k * k // TB, TB), jnp.float32)
    grams = pl.pallas_call(
        functools.partial(gram_kernel, 1.0 / (width * devices)),
        out_shape=packed,
        in_specs=[VECTORS] * CHUNKS,
        out_specs=VECTORS,
        name="gram",
    )(*current)
    grams = lax.all_to_all(grams, ("row", "col"), 0, 0, tiled=True)
    gram = pl.pallas_call(
        gram_sum_kernel,
        out_shape=jax.ShapeDtypeStruct((k, k), jnp.float32),
        in_specs=[VECTORS],
        out_specs=VECTORS,
        name="gram_sum",
    )(grams)
    return (jnp.concatenate(current, axis=0), gram)


def solution(mesh):
    in_specs = (
        P(None, ("row", "col")),
        P(("row", "col"), None, None),
        P(("row", "col"), None),
        P(("row", "col"), None),
    )
    out_specs = (P(None, ("row", "col")), P())
    return jax.shard_map(
        on_device, mesh=mesh, in_specs=in_specs, out_specs=out_specs, check_vma=False
    )
```

```python
import functools

import jax
import jax.numpy as jnp
from jax import lax
from jax.experimental import pallas as pl
from jax.experimental.pallas import tpu as pltpu
from jax.sharding import PartitionSpec as P

TB = 128
STEPS = 3
GROUP = 16
UNROLL = 32

SCALARS = pl.BlockSpec(memory_space=pltpu.SMEM)
VECTORS = pl.BlockSpec(memory_space=pltpu.VMEM)


def same_row(rows, index):
    return jnp.logical_and(index > 0, rows[index] == rows[jnp.maximum(index - 1, 0)])


def two_parts(value):
    high = value.astype(jnp.bfloat16)
    return high, (value - high.astype(jnp.float32)).astype(jnp.bfloat16)


def degree_kernel(rows, tiles_hbm, sent_ref, buffer, arrived):
    count = tiles_hbm.shape[0]
    groups = count // GROUP
    n_row, n_col, owned, _ = sent_ref.shape
    lane = lax.broadcasted_iota(jnp.int32, (TB, TB), 1)

    def fetch(group):
        at = pl.ds(group * GROUP, GROUP)
        return pltpu.make_async_copy(tiles_hbm.at[at], buffer.at[at], arrived.at[group])

    for group in range(groups):
        fetch(group).start()

    def body(group, total):
        fetch(group).wait()
        for t in range(GROUP):
            index = group * GROUP + t
            sums = jnp.sum(jnp.abs(buffer[index]), axis=1, keepdims=True)
            total = total + jnp.where(lane == rows[index], sums, 0.0)
        return total

    total = lax.fori_loop(0, groups, body, jnp.zeros((TB, TB), jnp.float32)).T
    for s in range(n_row):
        for d in range(n_col):
            sent_ref[s, d] = total[d * owned : (d + 1) * owned]


def degree_terms(tiles, rows, n_row, n_col, owned):
    count = tiles.shape[0]
    assert n_col * owned <= TB
    return pl.pallas_call(
        degree_kernel,
        out_shape=pltpu.VMEM((n_row, n_col, owned, TB), jnp.float32),
        in_specs=[SCALARS, pl.BlockSpec(memory_space=pltpu.HBM)],
        out_specs=VECTORS,
        scratch_shapes=[
            pltpu.VMEM(tiles.shape, jnp.float32),
            pltpu.SemaphoreType.DMA((count // GROUP,)),
        ],
        compiler_params=pltpu.CompilerParams(vmem_limit_bytes=24 << 20),
        cost_estimate=pl.CostEstimate(
            flops=count * TB * TB * 2, bytes_accessed=count * TB * TB * 4, transcendentals=0
        ),
        name="degree_terms",
    )(
        pltpu.with_memory_space_constraint(rows, pltpu.HBM),
        pltpu.with_memory_space_constraint(tiles, pltpu.HBM),
    )


def product_kernel(n_row, n_col, owned, load, rows, cols, place, *refs):
    refs = list(refs)
    take = lambda n: [refs.pop(0) for _ in range(n)]
    sources = take(n_row)
    terms_ref, tiles_from, keep_ref, give_ref, scale_ref = take(5)
    tiles_ref = refs.pop(0) if load else tiles_from
    operand, sums = take(2)
    count = tiles_ref.shape[0]
    k = keep_ref.shape[1]
    a, b = place[0], place[1]

    def fetch(group):
        at = pl.ds(group * UNROLL, UNROLL)
        return pltpu.make_async_copy(tiles_from.at[at], tiles_ref.at[at], refs[0].at[group])

    if load:
        for group in range(count // UNROLL):
            fetch(group).start()
    for s in range(n_row):
        degree = 1.0 + jnp.sum(terms_ref[a ^ s], axis=0)
        scale = 1.0 / jnp.sqrt(degree)
        for o in range(owned):
            at = slice(o * TB, (o + 1) * TB)
            if s == 0:
                scale_ref[:, at] = scale[o : o + 1]
            parts = two_parts(sources[s][:, at] * scale[o : o + 1])
            for i, value in enumerate(parts):
                operand[s * owned + o, i * k : (i + 1) * k, 0:TB] = value
                operand[s * owned + o, i * k : (i + 1) * k, TB : 2 * TB] = value

    def body(group, total):
        if load:
            fetch(group).wait()
        for t in range(UNROLL):
            index = group * UNROLL + t
            row, col = rows[index], cols[index]
            where_from = (lax.div(col, owned) ^ a) * owned + lax.rem(col, owned)
            where_to = (lax.div(row, owned) ^ b) * owned + lax.rem(row, owned)
            both = lax.dot_general(
                operand[where_from],
                jnp.concatenate(two_parts(tiles_ref[index]), axis=1),
                (((1,), (1,)), ((), ())),
                preferred_element_type=jnp.float32,
            )
            total = both[0:k] + both[k : 2 * k] + jnp.where(same_row(rows, index), total, 0.0)
            sums[where_to] = total
        return total

    lax.fori_loop(0, count // UNROLL, body, jnp.zeros((k, TB), jnp.float32))
    for d in range(n_col):
        out = give_ref if d % 2 else keep_ref
        for o in range(owned):
            out[d // 2, :, o * TB : (o + 1) * TB] = sums[d * owned + o]


def products(sources, terms, tiles, rows, cols, place, n_row, n_col, load):
    k, width = sources[0].shape
    owned = width // TB
    count = tiles.shape[0]
    half = jax.ShapeDtypeStruct((n_col // 2, k, width), jnp.float32)
    loaded = [jax.ShapeDtypeStruct(tiles.shape, tiles.dtype)] * load
    if load:
        tiles = pltpu.with_memory_space_constraint(tiles, pltpu.HBM)
    return pl.pallas_call(
        functools.partial(product_kernel, n_row, n_col, owned, load),
        out_shape=[half, half, jax.ShapeDtypeStruct((1, width), jnp.float32)] + loaded,
        in_specs=[SCALARS] * 3
        + [VECTORS] * (n_row + 1)
        + [pl.BlockSpec(memory_space=pltpu.HBM) if load else VECTORS],
        out_specs=[VECTORS] * (3 + load),
        scratch_shapes=[
            pltpu.VMEM((n_row * owned, 2 * k, 2 * TB), jnp.bfloat16),
            pltpu.VMEM((n_col * owned, k, TB), jnp.float32),
        ]
        + [pltpu.SemaphoreType.DMA((count // UNROLL,))] * load,
        compiler_params=pltpu.CompilerParams(vmem_limit_bytes=24 << 20),
        cost_estimate=pl.CostEstimate(
            flops=count * TB * TB * 2 * k * 4,
            bytes_accessed=count * TB * TB * 4,
            transcendentals=0,
        ),
        name="products",
    )(rows, cols, place, *sources, terms, tiles)


def finish_kernel(mean, value_ref, filtered_ref, gram_ref, sent):
    copy = pltpu.make_async_copy(value_ref, filtered_ref, sent)
    copy.start()
    value = value_ref[...]
    k = value.shape[0]
    parts = jnp.concatenate(two_parts(value), axis=0)
    gram = lax.dot_general(
        parts, parts, (((1,), (1,)), ((), ())), preferred_element_type=jnp.float32
    )
    gram = mean * (gram[:k, :k] + (gram[:k, k:] + gram[k:, :k]) + gram[k:, k:])
    rows = gram_ref.shape[1]
    packed = jnp.concatenate([gram[q * rows : (q + 1) * rows] for q in range(k // rows)], axis=1)
    for d in range(gram_ref.shape[0]):
        gram_ref[d] = packed
    copy.wait()


def gram_sum_kernel(parts_ref, out_ref):
    total = jnp.sum(parts_ref[...], axis=0)
    k = out_ref.shape[0]
    rows = total.shape[0]
    for q in range(k // rows):
        out_ref[q * rows : (q + 1) * rows, :] = total[:, q * k : (q + 1) * k]


def swap(value, axis, size, by):
    return lax.ppermute(value, axis, [(i, i ^ by) for i in range(size)])


def on_device(vectors, tiles, tile_row, tile_col):
    rows, cols = tile_row[0], tile_col[0]
    n_row = lax.axis_size("row")
    n_col = lax.axis_size("col")
    devices = n_row * n_col
    k, width = vectors.shape
    owned = width // TB
    place = jnp.stack([lax.axis_index("row"), lax.axis_index("col")]).astype(jnp.int32)

    def spread(value):
        return [value] + [swap(value, "row", n_row, s) for s in reversed(range(1, n_row))][::-1]

    sources = spread(vectors)
    sent = degree_terms(tiles, rows, n_row, n_col, owned)
    sent, sources = lax.optimization_barrier((sent, sources))
    terms = lax.all_to_all(
        sent.reshape(devices, owned, TB), ("row", "col"), 0, 0, tiled=True
    ).reshape(n_row, n_col, owned, TB)

    previous, current = None, vectors
    for step in range(STEPS):
        keep, give, scale, *loaded = products(
            sources, terms, tiles, rows, cols, place, n_row, n_col, step == 0
        )
        if loaded:
            tiles = loaded[0]
        chip = keep + swap(give, "col", n_col, 1)
        totals = [chip[0]] + [
            swap(chip[j], "col", n_col, 2 * j) for j in reversed(range(1, n_col // 2))
        ]
        following = sum(totals[1:], totals[0]) * scale
        if step > 0:
            following = 2.0 * following - previous
        previous, current = current, following
        if step < STEPS - 1:
            sources = spread(current)

    filtered, grams = pl.pallas_call(
        functools.partial(finish_kernel, 1.0 / (width * devices)),
        out_shape=[
            jax.ShapeDtypeStruct((k, width), jnp.float32),
            pltpu.VMEM((devices, k * k // TB, TB), jnp.float32),
        ],
        in_specs=[VECTORS],
        out_specs=[pl.BlockSpec(memory_space=pltpu.HBM), VECTORS],
        scratch_shapes=[pltpu.SemaphoreType.DMA],
        name="finish",
    )(pltpu.with_memory_space_constraint(current, pltpu.VMEM))
    grams = lax.all_to_all(grams, ("row", "col"), 0, 0, tiled=True)
    gram = pl.pallas_call(
        gram_sum_kernel,
        out_shape=jax.ShapeDtypeStruct((k, k), jnp.float32),
        in_specs=[VECTORS],
        out_specs=VECTORS,
        name="gram_sum",
    )(pltpu.with_memory_space_constraint(grams, pltpu.VMEM))
    return (filtered, gram)


def solution(mesh):
    in_specs = (
        P(None, ("row", "col")),
        P(("row", "col"), None, None),
        P(("row", "col"), None),
        P(("row", "col"), None),
    )
    out_specs = (P(None, ("row", "col")), P())
    return jax.shard_map(
        on_device, mesh=mesh, in_specs=in_specs, out_specs=out_specs, check_vma=False
    )
```

```python
import functools

import jax
import jax.numpy as jnp
from jax import lax
from jax.experimental import pallas as pl
from jax.experimental.pallas import tpu as pltpu
from jax.sharding import PartitionSpec as P

TB = 128
STEPS = 3
GROUP = 16
UNROLL = 32

SCALARS = pl.BlockSpec(memory_space=pltpu.SMEM)
VECTORS = pl.BlockSpec(memory_space=pltpu.VMEM)


def same_row(rows, index):
    return jnp.logical_and(index > 0, rows[index] == rows[jnp.maximum(index - 1, 0)])


def two_parts(value):
    high = value.astype(jnp.bfloat16)
    return high, (value - high.astype(jnp.float32)).astype(jnp.bfloat16)


def degree_kernel(rows, tiles_hbm, sent_ref, buffer, terms, arrived):
    count = tiles_hbm.shape[0]
    groups = count // GROUP
    n_row, n_col, owned, _ = sent_ref.shape
    lane = lax.broadcasted_iota(jnp.int32, (TB, TB), 1)
    ones = jnp.ones((16, 2 * TB), jnp.bfloat16)
    terms[...] = jnp.zeros_like(terms)

    def fetch(group):
        at = pl.ds(group * GROUP, GROUP)
        return pltpu.make_async_copy(tiles_hbm.at[at], buffer.at[at], arrived.at[group])

    for group in range(groups):
        fetch(group).start()

    def body(group, total):
        fetch(group).wait()
        for t in range(0, GROUP, 2):
            index = group * GROUP + t
            sums = jnp.sum(jnp.abs(buffer[index]), axis=1, keepdims=True)
            total = total + jnp.where(lane == rows[index], sums, 0.0)
            sums = lax.dot_general(
                ones,
                jnp.concatenate(two_parts(jnp.abs(buffer[index + 1])), axis=1),
                (((1,), (1,)), ((), ())),
                preferred_element_type=jnp.float32,
            )
            at = pl.ds(rows[index + 1], 1)
            terms[at, :] = terms[at, :] + sums[0:1]
        return total

    total = lax.fori_loop(0, groups, body, jnp.zeros((TB, TB), jnp.float32)).T
    for s in range(n_row):
        for d in range(n_col):
            at = slice(d * owned, (d + 1) * owned)
            sent_ref[s, d] = total[at] + terms[at]


def degree_terms(tiles, rows, n_row, n_col, owned):
    count = tiles.shape[0]
    assert n_col * owned <= TB
    return pl.pallas_call(
        degree_kernel,
        out_shape=pltpu.VMEM((n_row, n_col, owned, TB), jnp.float32),
        in_specs=[SCALARS, pl.BlockSpec(memory_space=pltpu.HBM)],
        out_specs=VECTORS,
        scratch_shapes=[
            pltpu.VMEM(tiles.shape, jnp.float32),
            pltpu.VMEM((n_col * owned, TB), jnp.float32),
            pltpu.SemaphoreType.DMA((count // GROUP,)),
        ],
        compiler_params=pltpu.CompilerParams(vmem_limit_bytes=24 << 20),
        cost_estimate=pl.CostEstimate(
            flops=count * TB * TB * 2, bytes_accessed=count * TB * TB * 4, transcendentals=0
        ),
        name="degree_terms",
    )(
        pltpu.with_memory_space_constraint(rows, pltpu.HBM),
        pltpu.with_memory_space_constraint(tiles, pltpu.HBM),
    )


def product_kernel(n_row, n_col, owned, load, unroll, rows, cols, place, *refs):
    refs = list(refs)
    take = lambda n: [refs.pop(0) for _ in range(n)]
    sources = take(n_row)
    terms_ref, tiles_from, keep_ref, give_ref, scale_ref = take(5)
    tiles_ref = refs.pop(0) if load else tiles_from
    operand, sums = take(2)
    count = tiles_ref.shape[0]
    k = keep_ref.shape[1]
    a, b = place[0], place[1]

    def fetch(group):
        at = pl.ds(group * unroll, unroll)
        return pltpu.make_async_copy(tiles_from.at[at], tiles_ref.at[at], refs[0].at[group])

    if load:
        for group in range(count // unroll):
            fetch(group).start()
    for s in range(n_row):
        degree = 1.0 + jnp.sum(terms_ref[a ^ s], axis=0)
        scale = 1.0 / jnp.sqrt(degree)
        for o in range(owned):
            at = slice(o * TB, (o + 1) * TB)
            if s == 0:
                scale_ref[:, at] = scale[o : o + 1]
            parts = two_parts(sources[s][:, at] * scale[o : o + 1])
            for i, value in enumerate(parts):
                operand[s * owned + o, i * k : (i + 1) * k, 0:TB] = value
                operand[s * owned + o, i * k : (i + 1) * k, TB : 2 * TB] = value

    def body(group, total):
        if load:
            fetch(group).wait()
        for t in range(unroll):
            index = group * unroll + t
            row, col = rows[index], cols[index]
            where_from = (lax.div(col, owned) ^ a) * owned + lax.rem(col, owned)
            where_to = (lax.div(row, owned) ^ b) * owned + lax.rem(row, owned)
            both = lax.dot_general(
                operand[where_from],
                jnp.concatenate(two_parts(tiles_ref[index]), axis=1),
                (((1,), (1,)), ((), ())),
                preferred_element_type=jnp.float32,
            )
            total = both[0:k] + both[k : 2 * k] + jnp.where(same_row(rows, index), total, 0.0)
            sums[where_to] = total
        return total

    lax.fori_loop(0, count // unroll, body, jnp.zeros((k, TB), jnp.float32))
    for d in range(n_col):
        out = give_ref if d % 2 else keep_ref
        for o in range(owned):
            out[d // 2, :, o * TB : (o + 1) * TB] = sums[d * owned + o]


def products(sources, terms, tiles, rows, cols, place, n_row, n_col, load):
    k, width = sources[0].shape
    owned = width // TB
    count = tiles.shape[0]
    half = jax.ShapeDtypeStruct((n_col // 2, k, width), jnp.float32)
    unroll = UNROLL if load else min(count, 4 * UNROLL)
    loaded = [jax.ShapeDtypeStruct(tiles.shape, tiles.dtype)] * load
    if load:
        tiles = pltpu.with_memory_space_constraint(tiles, pltpu.HBM)
    return pl.pallas_call(
        functools.partial(product_kernel, n_row, n_col, owned, load, unroll),
        out_shape=[half, half, jax.ShapeDtypeStruct((1, width), jnp.float32)] + loaded,
        in_specs=[SCALARS] * 3
        + [VECTORS] * (n_row + 1)
        + [pl.BlockSpec(memory_space=pltpu.HBM) if load else VECTORS],
        out_specs=[VECTORS] * (3 + load),
        scratch_shapes=[
            pltpu.VMEM((n_row * owned, 2 * k, 2 * TB), jnp.bfloat16),
            pltpu.VMEM((n_col * owned, k, TB), jnp.float32),
        ]
        + [pltpu.SemaphoreType.DMA((count // unroll,))] * load,
        compiler_params=pltpu.CompilerParams(vmem_limit_bytes=24 << 20),
        cost_estimate=pl.CostEstimate(
            flops=count * TB * TB * 2 * k * 4,
            bytes_accessed=count * TB * TB * 4,
            transcendentals=0,
        ),
        name="products",
    )(rows, cols, place, *sources, terms, tiles)


def finish_kernel(mean, value_ref, filtered_ref, gram_ref, sent):
    copy = pltpu.make_async_copy(value_ref, filtered_ref, sent)
    copy.start()
    value = value_ref[...]
    k = value.shape[0]
    parts = jnp.concatenate(two_parts(value), axis=0)
    gram = lax.dot_general(
        parts, parts, (((1,), (1,)), ((), ())), preferred_element_type=jnp.float32
    )
    gram = mean * (gram[:k, :k] + (gram[:k, k:] + gram[k:, :k]) + gram[k:, k:])
    rows = gram_ref.shape[1]
    packed = jnp.concatenate([gram[q * rows : (q + 1) * rows] for q in range(k // rows)], axis=1)
    for d in range(gram_ref.shape[0]):
        gram_ref[d] = packed
    copy.wait()


def gram_sum_kernel(parts_ref, out_ref):
    total = jnp.sum(parts_ref[...], axis=0)
    k = out_ref.shape[0]
    rows = total.shape[0]
    for q in range(k // rows):
        out_ref[q * rows : (q + 1) * rows, :] = total[:, q * k : (q + 1) * k]


def swap(value, axis, size, by):
    return lax.ppermute(value, axis, [(i, i ^ by) for i in range(size)])


def on_device(vectors, tiles, tile_row, tile_col):
    rows, cols = tile_row[0], tile_col[0]
    n_row = lax.axis_size("row")
    n_col = lax.axis_size("col")
    devices = n_row * n_col
    k, width = vectors.shape
    owned = width // TB
    place = jnp.stack([lax.axis_index("row"), lax.axis_index("col")]).astype(jnp.int32)

    def spread(value):
        return [value] + [swap(value, "row", n_row, s) for s in reversed(range(1, n_row))][::-1]

    sources = spread(vectors)
    sent = degree_terms(tiles, rows, n_row, n_col, owned)
    sent, sources = lax.optimization_barrier((sent, sources))
    terms = lax.all_to_all(
        sent.reshape(devices, owned, TB), ("row", "col"), 0, 0, tiled=True
    ).reshape(n_row, n_col, owned, TB)

    previous, current = None, vectors
    for step in range(STEPS):
        keep, give, scale, *loaded = products(
            sources, terms, tiles, rows, cols, place, n_row, n_col, step == 0
        )
        if loaded:
            tiles = loaded[0]
        chip = keep + swap(give, "col", n_col, 1)
        totals = [chip[0]] + [
            swap(chip[j], "col", n_col, 2 * j) for j in reversed(range(1, n_col // 2))
        ]
        following = sum(totals[1:], totals[0]) * scale
        if step > 0:
            following = 2.0 * following - previous
        previous, current = current, following
        if step < STEPS - 1:
            sources = spread(current)

    filtered, grams = pl.pallas_call(
        functools.partial(finish_kernel, 1.0 / (width * devices)),
        out_shape=[
            jax.ShapeDtypeStruct((k, width), jnp.float32),
            pltpu.VMEM((devices, k * k // TB, TB), jnp.float32),
        ],
        in_specs=[VECTORS],
        out_specs=[pl.BlockSpec(memory_space=pltpu.HBM), VECTORS],
        scratch_shapes=[pltpu.SemaphoreType.DMA],
        name="finish",
    )(pltpu.with_memory_space_constraint(current, pltpu.VMEM))
    grams = lax.all_to_all(grams, ("row", "col"), 0, 0, tiled=True)
    gram = pl.pallas_call(
        gram_sum_kernel,
        out_shape=jax.ShapeDtypeStruct((k, k), jnp.float32),
        in_specs=[VECTORS],
        out_specs=VECTORS,
        name="gram_sum",
    )(pltpu.with_memory_space_constraint(grams, pltpu.VMEM))
    return (filtered, gram)


def solution(mesh):
    in_specs = (
        P(None, ("row", "col")),
        P(("row", "col"), None, None),
        P(("row", "col"), None),
        P(("row", "col"), None),
    )
    out_specs = (P(None, ("row", "col")), P())
    return jax.shard_map(
        on_device, mesh=mesh, in_specs=in_specs, out_specs=out_specs, check_vma=False
    )
```

```python
import functools

import jax
import jax.numpy as jnp
from jax import lax
from jax.experimental import pallas as pl
from jax.experimental.pallas import tpu as pltpu
from jax.sharding import PartitionSpec as P

TB = 128
STEPS = 3
GROUP = 16
UNROLL = 32

SCALARS = pl.BlockSpec(memory_space=pltpu.SMEM)
VECTORS = pl.BlockSpec(memory_space=pltpu.VMEM)


def same_row(rows, index):
    return jnp.logical_and(index > 0, rows[index] == rows[jnp.maximum(index - 1, 0)])


def two_parts(value):
    high = value.astype(jnp.bfloat16)
    return high, (value - high.astype(jnp.float32)).astype(jnp.bfloat16)


def degree_kernel(rows, tiles_hbm, sent_ref, buffer, terms, arrived):
    count = tiles_hbm.shape[0]
    groups = count // GROUP
    n_row, n_col, owned, _ = sent_ref.shape
    lane = lax.broadcasted_iota(jnp.int32, (TB, TB), 1)
    ones = jnp.ones((16, 2 * TB), jnp.bfloat16)
    terms[...] = jnp.zeros_like(terms)

    def fetch(group):
        at = pl.ds(group * GROUP, GROUP)
        return pltpu.make_async_copy(tiles_hbm.at[at], buffer.at[at], arrived.at[group])

    for group in range(groups):
        fetch(group).start()

    def body(group, total):
        fetch(group).wait()
        for t in range(0, GROUP, 2):
            index = group * GROUP + t
            sums = jnp.sum(jnp.abs(buffer[index]), axis=1, keepdims=True)
            total = total + jnp.where(lane == rows[index], sums, 0.0)
            sums = lax.dot_general(
                ones,
                jnp.concatenate(two_parts(jnp.abs(buffer[index + 1])), axis=1),
                (((1,), (1,)), ((), ())),
                preferred_element_type=jnp.float32,
            )
            at = pl.ds(rows[index + 1], 1)
            terms[at, :] = terms[at, :] + sums[0:1]
        return total

    total = lax.fori_loop(0, groups, body, jnp.zeros((TB, TB), jnp.float32)).T
    for s in range(n_row):
        for d in range(n_col):
            at = slice(d * owned, (d + 1) * owned)
            sent_ref[s, d] = total[at] + terms[at]


def degree_terms(tiles, rows, n_row, n_col, owned):
    count = tiles.shape[0]
    assert n_col * owned <= TB
    return pl.pallas_call(
        degree_kernel,
        out_shape=pltpu.VMEM((n_row, n_col, owned, TB), jnp.float32),
        in_specs=[SCALARS, pl.BlockSpec(memory_space=pltpu.HBM)],
        out_specs=VECTORS,
        scratch_shapes=[
            pltpu.VMEM(tiles.shape, jnp.float32),
            pltpu.VMEM((n_col * owned, TB), jnp.float32),
            pltpu.SemaphoreType.DMA((count // GROUP,)),
        ],
        compiler_params=pltpu.CompilerParams(vmem_limit_bytes=24 << 20),
        cost_estimate=pl.CostEstimate(
            flops=count * TB * TB * 2, bytes_accessed=count * TB * TB * 4, transcendentals=0
        ),
        name="degree_terms",
    )(
        pltpu.with_memory_space_constraint(rows, pltpu.HBM),
        pltpu.with_memory_space_constraint(tiles, pltpu.HBM),
    )


def product_kernel(n_row, n_col, owned, load, unroll, rows, cols, place, *refs):
    refs = list(refs)
    take = lambda n: [refs.pop(0) for _ in range(n)]
    sources = take(n_row)
    terms_ref, tiles_from, keep_ref, give_ref, scale_ref = take(5)
    tiles_ref = refs.pop(0) if load else tiles_from
    operand, sums = take(2)
    count = tiles_ref.shape[0]
    k = keep_ref.shape[1]
    a, b = place[0], place[1]

    def fetch(group):
        at = pl.ds(group * unroll, unroll)
        return pltpu.make_async_copy(tiles_from.at[at], tiles_ref.at[at], refs[0].at[group])

    if load:
        for group in range(count // unroll):
            fetch(group).start()
    for s in range(n_row):
        degree = 1.0 + jnp.sum(terms_ref[a ^ s], axis=0)
        scale = 1.0 / jnp.sqrt(degree)
        for o in range(owned):
            at = slice(o * TB, (o + 1) * TB)
            if s == 0:
                scale_ref[:, at] = scale[o : o + 1]
            parts = two_parts(sources[s][:, at] * scale[o : o + 1])
            for i, value in enumerate(parts):
                operand[s * owned + o, i * k : (i + 1) * k, 0:TB] = value
                operand[s * owned + o, i * k : (i + 1) * k, TB : 2 * TB] = value

    def body(group, total):
        if load:
            fetch(group).wait()
        for t in range(unroll):
            index = group * unroll + t
            row, col = rows[index], cols[index]
            where_from = (lax.div(col, owned) ^ a) * owned + lax.rem(col, owned)
            where_to = (lax.div(row, owned) ^ b) * owned + lax.rem(row, owned)
            both = lax.dot_general(
                operand[where_from],
                jnp.concatenate(two_parts(tiles_ref[index]), axis=1),
                (((1,), (1,)), ((), ())),
                preferred_element_type=jnp.float32,
            )
            total = both[0:k] + both[k : 2 * k] + jnp.where(same_row(rows, index), total, 0.0)
            sums[where_to] = total
        return total

    lax.fori_loop(0, count // unroll, body, jnp.zeros((k, TB), jnp.float32))
    for d in range(n_col):
        out = give_ref if d % 2 else keep_ref
        for o in range(owned):
            out[d // 2, :, o * TB : (o + 1) * TB] = sums[d * owned + o]


def products(sources, terms, tiles, rows, cols, place, n_row, n_col, load):
    k, width = sources[0].shape
    owned = width // TB
    count = tiles.shape[0]
    half = jax.ShapeDtypeStruct((n_col // 2, k, width), jnp.float32)
    unroll = UNROLL if load else min(count, 4 * UNROLL)
    loaded = [jax.ShapeDtypeStruct(tiles.shape, tiles.dtype)] * load
    if load:
        tiles = pltpu.with_memory_space_constraint(tiles, pltpu.HBM)
    return pl.pallas_call(
        functools.partial(product_kernel, n_row, n_col, owned, load, unroll),
        out_shape=[half, half, jax.ShapeDtypeStruct((1, width), jnp.float32)] + loaded,
        in_specs=[SCALARS] * 3
        + [VECTORS] * (n_row + 1)
        + [pl.BlockSpec(memory_space=pltpu.HBM) if load else VECTORS],
        out_specs=[VECTORS] * (3 + load),
        scratch_shapes=[
            pltpu.VMEM((n_row * owned, 2 * k, 2 * TB), jnp.bfloat16),
            pltpu.VMEM((n_col * owned, k, TB), jnp.float32),
        ]
        + [pltpu.SemaphoreType.DMA((count // unroll,))] * load,
        compiler_params=pltpu.CompilerParams(vmem_limit_bytes=24 << 20),
        cost_estimate=pl.CostEstimate(
            flops=count * TB * TB * 2 * k * 4,
            bytes_accessed=count * TB * TB * 4,
            transcendentals=0,
        ),
        name="products",
    )(rows, cols, place, *sources, terms, tiles)


def finish_kernel(mean, value_ref, filtered_ref, gram_ref, sent):
    copy = pltpu.make_async_copy(value_ref, filtered_ref, sent)
    copy.start()
    value = value_ref[...]
    k = value.shape[0]
    parts = jnp.concatenate(two_parts(value), axis=0)
    gram = lax.dot_general(
        parts, parts, (((1,), (1,)), ((), ())), preferred_element_type=jnp.float32
    )
    gram = mean * (gram[:k, :k] + (gram[:k, k:] + gram[k:, :k]) + gram[k:, k:])
    rows = gram_ref.shape[1]
    packed = jnp.concatenate([gram[q * rows : (q + 1) * rows] for q in range(k // rows)], axis=1)
    for d in range(gram_ref.shape[0]):
        gram_ref[d] = packed
    copy.wait()


def gram_sum_kernel(parts_ref, out_ref):
    total = jnp.sum(parts_ref[...], axis=0)
    k = out_ref.shape[0]
    rows = total.shape[0]
    for q in range(k // rows):
        out_ref[q * rows : (q + 1) * rows, :] = total[:, q * k : (q + 1) * k]


def swap(value, axis, size, by):
    return lax.ppermute(value, axis, [(i, i ^ by) for i in range(size)])


def on_device(vectors, tiles, tile_row, tile_col):
    rows, cols = tile_row[0], tile_col[0]
    n_row = lax.axis_size("row")
    n_col = lax.axis_size("col")
    devices = n_row * n_col
    k, width = vectors.shape
    owned = width // TB
    place = jnp.stack([lax.axis_index("row"), lax.axis_index("col")]).astype(jnp.int32)

    def spread(value):
        return [value] + [swap(value, "row", n_row, s) for s in reversed(range(1, n_row))][::-1]

    sources = spread(vectors)
    sent = degree_terms(tiles, rows, n_row, n_col, owned)
    sent, sources = lax.optimization_barrier((sent, sources))
    terms = lax.all_to_all(
        sent.reshape(devices, owned, TB), ("row", "col"), 0, 0, tiled=True
    ).reshape(n_row, n_col, owned, TB)

    previous, current = None, vectors
    for step in range(STEPS):
        keep, give, scale, *loaded = products(
            sources, terms, tiles, rows, cols, place, n_row, n_col, step == 0
        )
        if loaded:
            tiles = loaded[0]
        chip = keep + swap(give, "col", n_col, 1)
        if n_col == 8:
            half = k // 2
            passed = swap(chip[3, :half], "col", n_col, 2)
            across = swap(chip[3, half:], "col", n_col, 6)
            second = swap(chip[2, half:], "col", n_col, 4)
            merged = swap(chip[2, :half] + passed, "col", n_col, 4)
            first = swap(chip[1], "col", n_col, 2)
            total = chip[0] + first + jnp.concatenate([merged, second + across], axis=0)
        else:
            total = chip[0]
            for j in reversed(range(1, n_col // 2)):
                total = total + swap(chip[j], "col", n_col, 2 * j)
        following = total * scale
        if step > 0:
            following = 2.0 * following - previous
        previous, current = current, following
        if step < STEPS - 1:
            sources = spread(current)

    filtered, grams = pl.pallas_call(
        functools.partial(finish_kernel, 1.0 / (width * devices)),
        out_shape=[
            jax.ShapeDtypeStruct((k, width), jnp.float32),
            pltpu.VMEM((devices, k * k // TB, TB), jnp.float32),
        ],
        in_specs=[VECTORS],
        out_specs=[pl.BlockSpec(memory_space=pltpu.HBM), VECTORS],
        scratch_shapes=[pltpu.SemaphoreType.DMA],
        name="finish",
    )(pltpu.with_memory_space_constraint(current, pltpu.VMEM))
    grams = lax.all_to_all(grams, ("row", "col"), 0, 0, tiled=True)
    gram = pl.pallas_call(
        gram_sum_kernel,
        out_shape=jax.ShapeDtypeStruct((k, k), jnp.float32),
        in_specs=[VECTORS],
        out_specs=VECTORS,
        name="gram_sum",
    )(pltpu.with_memory_space_constraint(grams, pltpu.VMEM))
    return (filtered, gram)


def solution(mesh):
    in_specs = (
        P(None, ("row", "col")),
        P(("row", "col"), None, None),
        P(("row", "col"), None),
        P(("row", "col"), None),
    )
    out_specs = (P(None, ("row", "col")), P())
    return jax.shard_map(
        on_device, mesh=mesh, in_specs=in_specs, out_specs=out_specs, check_vma=False
    )
```
